128 devices in a mesh: seg: 16 (over z, y), dev: 8 (over x, core).
Axes of the slice: x: 4, y: 4, z: 4, core: 2. Of those that a mesh axis runs over, the one named last changes fastest.
Arguments:
- queries: bfloat16 [16384, 4096], P(('seg', 'dev')), may hold values from -10 to 10
- keys: bfloat16 [16384, 1024], P(('seg', 'dev')), may hold values from -10 to 10
- values: bfloat16 [16384, 1024], P(('seg', 'dev')), may hold values from -6 to 6
- doc_start: int32 [16384], P(('seg', 'dev')), may hold values from 0 to 15872, as said below
Outputs:
- attended: bfloat16 [16384, 4096], P(('seg', 'dev'))
- log_totals: float32 [32, 16384], P(None, ('seg', 'dev'))
The draws below stay inside these ranges and needn't reach their ends.
Inputs may be any that keep to these rules, and one draw needn't show every extreme that they name: doc_start is non-decreasing, doc_start[i] <= i and i - doc_start[i] < 512; doc_start[i] = i where a document begins. The last document is the last 512 tokens; the one before it has 1 to 512 tokens; every earlier document has 128 to 512 tokens.
All inputs are finite; a program needn't handle non-finite values.
Results may differ from the reference program's by a relative error of at most 0.004.
Values may be sent and summed in bfloat16 or wider, within the bound.
No kernel may reach another device: no remote copies, remote signals or barrier semaphores. Data moves between devices by JAX's collectives and lax.ppermute only.
A program may use at most 64 MiB of HBM per device.

```python
import math
import jax
import jax.numpy as jnp
from jax import lax

HEADS = 32
KV_HEADS = 8
HEAD_DIM = 128
TOK_DEV = 128
BACK = 4
GROUP = 4
TOKENS = 16384


def draw_queries(key, part):
    shape = (TOKENS, HEADS * HEAD_DIM)
    field = jnp.clip(jax.random.normal(jax.random.fold_in(key, 2), shape), -6.0, 6.0)
    return field.astype(jnp.bfloat16)


def draw_keys(key, part):
    shape = (TOKENS, KV_HEADS * HEAD_DIM)
    field = jnp.clip(jax.random.normal(jax.random.fold_in(key, 4), shape), -6.0, 6.0)
    return field.astype(jnp.bfloat16)


def draw_doc_start(key, part):
    doc_count = TOKENS // TOK_DEV + 1
    lengths = jax.random.randint(jax.random.fold_in(key, 11), (doc_count,), TOK_DEV, BACK * TOK_DEV + 1)
    ends = jnp.cumsum(lengths)
    starts = ends - lengths
    place = jnp.arange(TOKENS)
    inside = starts[None, :] <= place[:, None]
    found = jnp.max(jnp.where(inside, starts[None, :], 0), axis=1)
    last_start = TOKENS - BACK * TOK_DEV
    found = jnp.where(place >= last_start, last_start, found)
    return found.astype(jnp.int32)


def block_levels(rng, shape, cuts, least, largest):
    loudness, own = 1.0, jax.random.fold_in(rng, 6)
    for axis_at, parts in cuts:
        steps = jnp.exp(jax.random.uniform(jax.random.fold_in(own, axis_at), (parts,), jnp.float32, least / len(cuts), largest / len(cuts)))
        loudness = loudness * jnp.repeat(steps, shape[axis_at] // parts).reshape([-1 if axis == axis_at else 1 for axis in range(len(shape))])
    return loudness


def centred(rng, extent, width, most, pieces=(), kind=jnp.bfloat16):
    values = width * jax.random.normal(rng, extent, jnp.float32)
    if pieces:
        values = values * block_levels(rng, extent, pieces, -0.22, 0.18)
    return jnp.clip(values, -most, most).astype(kind)


def setup_inputs(seed: int = 0) -> dict:
    key_list = jax.random.split(jax.random.key(seed), 5)
    return {
        "queries": draw_queries(jax.random.fold_in(key_list[4], 71), 0),
        "keys": draw_keys(jax.random.fold_in(key_list[4], 71), 0),
        "values": centred(key_list[2], (TOKENS, KV_HEADS * HEAD_DIM), 1.0, 6.0, ((0, 128),)),
        "doc_start": draw_doc_start(jax.random.fold_in(key_list[4], 71), 0),
    }


LOWEST = -1e+30

def reference(queries, keys, values, doc_start):
    row_count = TOK_DEV
    reach_rows = BACK * row_count
    score_scale = 1.0 / math.sqrt(HEAD_DIM)
    padded_keys = jnp.concatenate([jnp.zeros((reach_rows, keys.shape[1]), keys.dtype), keys], axis=0)
    padded_values = jnp.concatenate([jnp.zeros((reach_rows, values.shape[1]), values.dtype), values], axis=0)

    def query_block(block_index):
        start = (block_index * row_count).astype(jnp.int32)
        query_rows = lax.dynamic_slice_in_dim(queries, start, row_count, 0)
        query_rows = query_rows.reshape(row_count, KV_HEADS, GROUP, HEAD_DIM).astype(jnp.float32)
        key_rows = lax.dynamic_slice_in_dim(padded_keys, start, reach_rows + row_count, 0)
        key_rows = key_rows.reshape(reach_rows + row_count, KV_HEADS, HEAD_DIM).astype(jnp.float32)
        value_rows = lax.dynamic_slice_in_dim(padded_values, start, reach_rows + row_count, 0)
        value_rows = value_rows.reshape(reach_rows + row_count, KV_HEADS, HEAD_DIM).astype(jnp.float32)
        starts_here = lax.dynamic_slice_in_dim(doc_start, start, row_count, 0)
        query_place = start + jnp.arange(row_count, dtype=jnp.int32)
        key_place = start - reach_rows + jnp.arange(reach_rows + row_count, dtype=jnp.int32)
        allowed = (key_place[None, :] >= starts_here[:, None]) & (key_place[None, :] <= query_place[:, None])
        scores = jnp.einsum('qgad,kgd->gaqk', query_rows, key_rows) * score_scale
        scores = jnp.where(allowed, scores, LOWEST)
        highest = lax.optimization_barrier(jnp.max(scores, axis=-1, keepdims=True))
        expos = jnp.where(allowed, jnp.exp(scores - highest), 0.0)
        totals = lax.optimization_barrier(jnp.sum(expos, axis=-1))
        rounded = lax.optimization_barrier(expos.astype(jnp.bfloat16)).astype(jnp.float32)
        summed = jnp.einsum('gaqk,kgd->qgad', rounded, value_rows)
        attended = summed / jnp.transpose(totals, (2, 0, 1))[..., None]
        attended = attended.reshape(row_count, HEADS * HEAD_DIM).astype(jnp.bfloat16)
        log_totals = (highest[..., 0] + jnp.log(totals)).reshape(HEADS, row_count)
        return (attended, log_totals)
    outputs, logs = lax.map(query_block, jnp.arange(TOKENS // row_count, dtype=jnp.int32))
    attended = outputs.reshape(TOKENS, HEADS * HEAD_DIM)
    log_totals = jnp.transpose(logs, (1, 0, 2)).reshape(HEADS, TOKENS)
    return (attended, log_totals)
```

```python
import functools
import math

import jax
import jax.numpy as jnp
from jax import lax
from jax.experimental import pallas as pl
from jax.experimental.pallas import tpu as pltpu
from jax.sharding import PartitionSpec as P

HEAD_DIM = 128
BACK = 4
LOWEST = -1e30
SCALE = 1.0 / math.sqrt(HEAD_DIM)
LOG2E = math.log2(math.e)
AXES = ("seg", "dev")


def attend_kernel(
    pairs, group, first_ref, doc_ref, q_ref, own_k, own_v, k1, k2, k3, k4, v1, v2, v3, v4,
    out_ref, log_ref, bias_ref,
):
    rows = q_ref.shape[0]
    row = lax.broadcasted_iota(jnp.int32, (rows, rows), 0)
    col = lax.broadcasted_iota(jnp.int32, (rows, rows), 1)
    causal = col <= row

    @pl.when(pl.program_id(0) == 0)
    def _():
        start = jnp.transpose(jnp.broadcast_to(doc_ref[...], (rows, rows))) - first_ref[0]
        place = jnp.where(causal, col, col - BACK * rows)
        bias_ref[0] = jnp.where(place >= start, 0.0, LOWEST)
        for back in range(1, BACK):
            bias_ref[back] = jnp.where(col - back * rows >= start, 0.0, LOWEST)

    lane = lax.broadcasted_iota(jnp.int32, (rows, HEAD_DIM), 1)
    logs = jnp.zeros((rows, HEAD_DIM), jnp.float32)
    for pair in range(pairs):
        lo = pair * HEAD_DIM
        at = slice(lo, lo + HEAD_DIM)
        key = jnp.concatenate([own_k[:, at], k4[:, at], k1[:, at], k2[:, at], k3[:, at]], axis=0)
        value = jnp.concatenate([own_v[:, at], v4[:, at], v1[:, at], v2[:, at], v3[:, at]], axis=0)
        for head in range(group):
            wide = (pair * group + head) * HEAD_DIM
            query = q_ref[:, wide : wide + HEAD_DIM]
            raw = lax.dot_general(
                query, key, (((1,), (1,)), ((), ())), preferred_element_type=jnp.float32
            )
            near = jnp.where(causal, raw[:, :rows], raw[:, rows : 2 * rows]) + bias_ref[0]
            tiles = [near] + [
                raw[:, (back + 1) * rows : (back + 2) * rows] + bias_ref[back]
                for back in range(1, BACK)
            ]
            top = jnp.max(functools.reduce(jnp.maximum, tiles), axis=1, keepdims=True)
            expos = [jnp.exp2((tile - top) * (SCALE * LOG2E)) for tile in tiles]
            total = jnp.sum(functools.reduce(jnp.add, expos), axis=1, keepdims=True)
            rounded = [e.astype(jnp.bfloat16) for e in expos]
            zero = jnp.zeros_like(rounded[0])
            weights = jnp.concatenate(
                [jnp.where(causal, rounded[0], zero), jnp.where(causal, zero, rounded[0])]
                + rounded[1:],
                axis=1,
            )
            summed = jnp.dot(weights, value, preferred_element_type=jnp.float32)
            out_ref[:, wide : wide + HEAD_DIM] = (summed * (1.0 / total)).astype(out_ref.dtype)
            log_total = top * SCALE + jnp.log(total)
            logs = jnp.where(lane == pair * group + head, log_total, logs)
    log_ref[...] = jnp.transpose(logs)[: pairs * group]


def attention(queries, own, blocks, doc_start, first_row):
    rows, width = queries.shape
    kv_heads = own[0].shape[1] // HEAD_DIM
    group = width // own[0].shape[1]
    pairs = 2
    steps = kv_heads // pairs
    narrow = pl.BlockSpec((rows, pairs * HEAD_DIM), lambda i: (0, i))
    wide = pl.BlockSpec((rows, pairs * group * HEAD_DIM), lambda i: (0, i))
    keys = [own[0], own[1]] + [b[0] for b in blocks] + [b[1] for b in blocks]
    return pl.pallas_call(
        functools.partial(attend_kernel, pairs, group),
        grid=(steps,),
        in_specs=[
            pl.BlockSpec(memory_space=pltpu.SMEM),
            pl.BlockSpec((1, rows), lambda i: (0, 0)),
            wide,
        ]
        + [narrow] * len(keys),
        out_specs=[wide, pl.BlockSpec((pairs * group, rows), lambda i: (i, 0))],
        out_shape=[
            jax.ShapeDtypeStruct((rows, width), jnp.bfloat16),
            jax.ShapeDtypeStruct((kv_heads * group, rows), jnp.float32),
        ],
        scratch_shapes=[pltpu.VMEM((BACK, rows, rows), jnp.float32)],
        name="attend",
    )(first_row, doc_start.reshape(1, rows), queries, *keys)


def local(queries, keys, values, doc_start):
    rows = queries.shape[0]
    devices = lax.axis_size(AXES)
    me = lax.axis_index(AXES)
    first_row = (me * rows).astype(jnp.int32).reshape(1)
    odd = (me % 2) == 1

    def shifted(x, by):
        return lax.ppermute(x, AXES, [(i, i + by) for i in range(devices) if i + by < devices])

    def swapped(x):
        return lax.ppermute(x, AXES, [(i, i ^ 1) for i in range(devices)])

    two = (shifted(keys, 2), shifted(values, 2))
    four = (shifted(keys, 4), shifted(values, 4))
    near = (swapped(keys), swapped(values))
    two_swap = (swapped(two[0]), swapped(two[1]))
    four_swap = (swapped(four[0]), swapped(four[1]))
    one = tuple(jnp.where(odd, a, b) for a, b in zip(near, two_swap))
    three = tuple(jnp.where(odd, a, b) for a, b in zip(two_swap, four_swap))
    blocks = [one, two, three, four]
    return tuple(attention(queries, (keys, values), blocks, doc_start, first_row))


def solution(mesh):
    placed = (P(AXES, None), P(AXES, None), P(AXES, None), P(AXES))
    return jax.shard_map(
        local,
        mesh=mesh,
        in_specs=placed,
        out_specs=(P(AXES, None), P(None, AXES)),
        check_vma=False,
    )
```

```python
import functools
import math

import jax
import jax.numpy as jnp
from jax import lax
from jax.experimental import pallas as pl
from jax.experimental.pallas import tpu as pltpu
from jax.sharding import PartitionSpec as P

HEAD_DIM = 128
BACK = 4
LOWEST = -1e30
SCALE = 1.0 / math.sqrt(HEAD_DIM)
LOG2E = math.log2(math.e)
AXES = ("seg", "dev")


def causal_tile(rows):
    key = lax.broadcasted_iota(jnp.int32, (rows, rows), 0)
    query = lax.broadcasted_iota(jnp.int32, (rows, rows), 1)
    return key <= query, key


def in_order(here_ref, blocks, at):
    own, near, two, two_swap, four, four_swap = (b[:, at] for b in blocks)
    odd = jnp.full(own.shape, here_ref[1], jnp.int32) == 1
    one = jnp.where(odd, near, two_swap)
    three = jnp.where(odd, two_swap, four_swap)
    return jnp.concatenate([own, four, one, two, three], axis=0)


def scores_kernel(pairs, group, here_ref, doc_ref, q_ref, *refs):
    blocks, (weight_ref, inverse_ref, log_ref, bias_ref) = refs[:6], refs[6:]
    rows = q_ref.shape[0]
    causal, place = causal_tile(rows)

    start = jnp.broadcast_to(doc_ref[...] - here_ref[0], (rows, rows))
    merged = jnp.where(causal, place, place - BACK * rows)
    bias_ref[0] = jnp.where(merged >= start, 0.0, LOWEST)
    for back in range(1, BACK):
        bias_ref[back] = jnp.where(place - back * rows >= start, 0.0, LOWEST)

    for pair in range(pairs):
        key = in_order(here_ref, blocks, slice(pair * HEAD_DIM, (pair + 1) * HEAD_DIM))
        for g in range(group):
            head = pair * group + g
            raw = lax.dot_general(
                key,
                q_ref[:, head * HEAD_DIM : (head + 1) * HEAD_DIM],
                (((1,), (1,)), ((), ())),
                preferred_element_type=jnp.float32,
            )
            tiles = [jnp.where(causal, raw[:rows], raw[rows : 2 * rows]) + bias_ref[0]] + [
                raw[(back + 1) * rows : (back + 2) * rows] + bias_ref[back]
                for back in range(1, BACK)
            ]
            top = jnp.max(functools.reduce(jnp.maximum, tiles), axis=0, keepdims=True)
            expos = [jnp.exp2((tile - top) * (SCALE * LOG2E)) for tile in tiles]
            total = jnp.sum(functools.reduce(jnp.add, expos), axis=0, keepdims=True)
            for index, e in enumerate(expos):
                weight_ref[
                    (pair * BACK + index) * rows : (pair * BACK + index + 1) * rows,
                    g * rows : (g + 1) * rows,
                ] = e.astype(jnp.bfloat16)
            log_ref[head : head + 1] = top * SCALE + jnp.log(total)
            inverse_ref[head : head + 1] = 1.0 / total


def values_kernel(pairs, group, here_ref, weight_ref, inverse_ref, *refs):
    blocks, out_ref = refs[:6], refs[6]
    rows = out_ref.shape[0]
    causal, _ = causal_tile(rows)
    causal = jnp.concatenate([causal] * group, axis=1)
    for pair in range(pairs):
        value = in_order(here_ref, blocks, slice(pair * HEAD_DIM, (pair + 1) * HEAD_DIM))
        weights = weight_ref[pair * BACK * rows : (pair + 1) * BACK * rows]
        near = weights[:rows]
        zero = jnp.zeros_like(near)
        weights = jnp.concatenate(
            [jnp.where(causal, near, zero), jnp.where(causal, zero, near), weights[rows:]], axis=0
        )
        summed = lax.dot_general(
            value, weights, (((0,), (0,)), ((), ())), preferred_element_type=jnp.float32
        )
        for g in range(group):
            head = pair * group + g
            out_ref[:, head * HEAD_DIM : (head + 1) * HEAD_DIM] = jnp.transpose(
                (summed[:, g * rows : (g + 1) * rows] * inverse_ref[head : head + 1]).astype(
                    out_ref.dtype
                )
            )


def weigh(queries, keys, doc_start, here):
    rows, width = queries.shape
    kv_heads = keys[0].shape[1] // HEAD_DIM
    group = width // keys[0].shape[1]
    heads = kv_heads * group
    reach = BACK * rows
    whole = pl.BlockSpec(memory_space=pltpu.VMEM)
    return pl.pallas_call(
        functools.partial(scores_kernel, kv_heads, group),
        in_specs=[pl.BlockSpec(memory_space=pltpu.SMEM)] + [whole] * 8,
        out_specs=[whole] * 3,
        out_shape=[
            jax.ShapeDtypeStruct((kv_heads * reach, group * rows), jnp.bfloat16),
            jax.ShapeDtypeStruct((heads, rows), jnp.float32),
            jax.ShapeDtypeStruct((heads, rows), jnp.float32),
        ],
        scratch_shapes=[pltpu.VMEM((BACK, rows, rows), jnp.float32)],
        cost_estimate=pl.CostEstimate(
            flops=2 * rows * (reach + rows) * width,
            bytes_accessed=8 << 20,
            transcendentals=rows * reach * heads,
        ),
        compiler_params=pltpu.CompilerParams(vmem_limit_bytes=32 << 20),
        name="scores",
    )(here, doc_start.reshape(1, rows), queries, *keys)


def combine(weights, inverses, values, here, width):
    rows = values[0].shape[0]
    kv_heads = values[0].shape[1] // HEAD_DIM
    group = width // values[0].shape[1]
    whole = pl.BlockSpec(memory_space=pltpu.VMEM)
    return pl.pallas_call(
        functools.partial(values_kernel, kv_heads, group),
        in_specs=[pl.BlockSpec(memory_space=pltpu.SMEM)] + [whole] * 8,
        out_specs=whole,
        out_shape=jax.ShapeDtypeStruct((rows, width), jnp.bfloat16),
        cost_estimate=pl.CostEstimate(
            flops=2 * rows * (BACK + 1) * rows * width, bytes_accessed=8 << 20, transcendentals=0
        ),
        compiler_params=pltpu.CompilerParams(vmem_limit_bytes=32 << 20),
        name="values",
    )(here, weights, inverses, *values)


def local(queries, keys, values, doc_start):
    rows, width = queries.shape
    devices = lax.axis_size(AXES)
    me = lax.axis_index(AXES)
    here = jnp.stack([me * rows, me % 2]).astype(jnp.int32)
    chain = devices - BACK

    def two_back(x):
        pairs = [(i, (i + 2) % chain) for i in range(chain)]
        pairs += [(chain + i, chain + (i + 2) % BACK) for i in range(BACK)]
        return lax.ppermute(x, AXES, pairs)

    def four_back(x):
        return lax.ppermute(x, AXES, [(i, i + 4) for i in range(chain - 4)])

    def swapped(x):
        return lax.ppermute(x, AXES, [(i, i ^ 1) for i in range(devices)])

    key_near = swapped(keys)
    key_two, key_four = two_back(keys), four_back(keys)
    value_two, value_four = two_back(values), four_back(values)
    value_near = swapped(values)
    key_two_swap, key_four_swap = lax.cond(
        doc_start[0] >= 0,
        lambda a, b: (swapped(a), swapped(b)),
        lambda a, b: (a, b),
        key_two,
        key_four,
    )
    all_keys = (keys, key_near, key_two, key_two_swap, key_four, key_four_swap)
    weights, inverses, logs = weigh(queries, all_keys, doc_start, here)
    value_two, value_four, weights = lax.optimization_barrier((value_two, value_four, weights))
    all_values = (
        values, value_near, value_two, swapped(value_two), value_four, swapped(value_four)
    )
    return combine(weights, inverses, all_values, here, width), logs


def solution(mesh):
    placed = (P(AXES, None), P(AXES, None), P(AXES, None), P(AXES))
    return jax.shard_map(
        local,
        mesh=mesh,
        in_specs=placed,
        out_specs=(P(AXES, None), P(None, AXES)),
        check_vma=False,
    )
```

```python
import functools
import math

import jax
import jax.numpy as jnp
from jax import lax
from jax.experimental import pallas as pl
from jax.experimental.pallas import tpu as pltpu
from jax.sharding import PartitionSpec as P

HEAD_DIM = 128
BACK = 4
LOWEST = -1e30
SCALE = 1.0 / math.sqrt(HEAD_DIM)
LOG2E = math.log2(math.e)
AXES = ("seg", "dev")


def causal_tile(rows):
    key = lax.broadcasted_iota(jnp.int32, (rows, rows), 0)
    query = lax.broadcasted_iota(jnp.int32, (rows, rows), 1)
    return key <= query, key


def in_order(here_ref, blocks, at):
    own, near, two, two_swap, four, four_swap = (b[:, at] for b in blocks)
    odd = jnp.full(own.shape, here_ref[1], jnp.int32) == 1
    one = jnp.where(odd, near, two_swap)
    three = jnp.where(odd, two_swap, four_swap)
    return jnp.concatenate([own, four, one, two, three], axis=0)


def scores_kernel(
    pairs, group, here_ref, near, two, four, doc_hbm, q_hbm, own_hbm, two_swap_hbm, four_swap_hbm,
    weight_ref, inverse_ref, log_ref, doc_ref, q_ref, own, two_swap, four_swap, bias_ref, sems,
):
    moves = [
        (doc_hbm, doc_ref),
        (own_hbm, own),
        (two_swap_hbm, two_swap),
        (four_swap_hbm, four_swap),
        (q_hbm, q_ref),
    ]
    copies = [
        pltpu.make_async_copy(source, target, sems.at[index])
        for index, (source, target) in enumerate(moves)
    ]
    for copy in copies:
        copy.start()
    rows = q_ref.shape[0]
    causal, place = causal_tile(rows)
    copies[0].wait()
    start = jnp.broadcast_to(doc_ref[...] - here_ref[0], (rows, rows))
    merged = jnp.where(causal, place, place - BACK * rows)
    bias_ref[0] = jnp.where(merged >= start, 0.0, LOWEST)
    for back in range(1, BACK):
        bias_ref[back] = jnp.where(place - back * rows >= start, 0.0, LOWEST)
    for copy in copies[1:]:
        copy.wait()

    blocks = (own, near, two, two_swap, four, four_swap)
    for pair in range(pairs):
        key = in_order(here_ref, blocks, slice(pair * HEAD_DIM, (pair + 1) * HEAD_DIM))
        for g in range(group):
            head = pair * group + g
            raw = lax.dot_general(
                key,
                q_ref[:, head * HEAD_DIM : (head + 1) * HEAD_DIM],
                (((1,), (1,)), ((), ())),
                preferred_element_type=jnp.float32,
            )
            tiles = [jnp.where(causal, raw[:rows], raw[rows : 2 * rows]) + bias_ref[0]] + [
                raw[(back + 1) * rows : (back + 2) * rows] + bias_ref[back]
                for back in range(1, BACK)
            ]
            top = jnp.max(functools.reduce(jnp.maximum, tiles), axis=0, keepdims=True)
            expos = [jnp.exp2((tile - top) * (SCALE * LOG2E)) for tile in tiles]
            total = jnp.sum(functools.reduce(jnp.add, expos), axis=0, keepdims=True)
            for index, e in enumerate(expos):
                weight_ref[
                    (pair * BACK + index) * rows : (pair * BACK + index + 1) * rows,
                    g * rows : (g + 1) * rows,
                ] = e.astype(jnp.bfloat16)
            log_ref[head : head + 1] = top * SCALE + jnp.log(total)
            inverse_ref[head : head + 1] = 1.0 / total


def values_kernel(pairs, group, here_ref, weight_ref, inverse_ref, *refs):
    blocks, (out_hbm, out_ref, sems) = refs[:6], refs[6:]
    rows = out_ref.shape[0]
    copies = []
    causal, _ = causal_tile(rows)
    causal = jnp.concatenate([causal] * group, axis=1)
    for pair in range(pairs):
        value = in_order(here_ref, blocks, slice(pair * HEAD_DIM, (pair + 1) * HEAD_DIM))
        weights = weight_ref[pair * BACK * rows : (pair + 1) * BACK * rows]
        near = weights[:rows]
        zero = jnp.zeros_like(near)
        weights = jnp.concatenate(
            [jnp.where(causal, near, zero), jnp.where(causal, zero, near), weights[rows:]], axis=0
        )
        summed = lax.dot_general(
            value, weights, (((0,), (0,)), ((), ())), preferred_element_type=jnp.float32
        )
        for g in range(group):
            head = pair * group + g
            out_ref[:, head * HEAD_DIM : (head + 1) * HEAD_DIM] = jnp.transpose(
                (summed[:, g * rows : (g + 1) * rows] * inverse_ref[head : head + 1]).astype(
                    out_ref.dtype
                )
            )
        part = pl.ds(pair * group * HEAD_DIM, group * HEAD_DIM)
        copies.append(
            pltpu.make_async_copy(out_ref.at[:, part], out_hbm.at[:, part], sems.at[pair])
        )
        copies[-1].start()
    for copy in copies:
        copy.wait()


def weigh(queries, keys, doc_start, here):
    rows, width = queries.shape
    kv_heads = keys[0].shape[1] // HEAD_DIM
    group = width // keys[0].shape[1]
    heads = kv_heads * group
    reach = BACK * rows
    whole = pl.BlockSpec(memory_space=pltpu.VMEM)
    left = pl.BlockSpec(memory_space=pltpu.HBM)
    own, near, two, two_swap, four, four_swap = keys
    brought = [doc_start.reshape(1, rows), queries, own, two_swap, four_swap]
    return pl.pallas_call(
        functools.partial(scores_kernel, kv_heads, group),
        in_specs=[pl.BlockSpec(memory_space=pltpu.SMEM)] + [whole] * 3 + [left] * 5,
        out_specs=[whole] * 3,
        out_shape=[
            jax.ShapeDtypeStruct((kv_heads * reach, group * rows), jnp.bfloat16),
            jax.ShapeDtypeStruct((heads, rows), jnp.float32),
            jax.ShapeDtypeStruct((heads, rows), jnp.float32),
        ],
        scratch_shapes=[pltpu.VMEM(x.shape, x.dtype) for x in brought]
        + [pltpu.VMEM((BACK, rows, rows), jnp.float32), pltpu.SemaphoreType.DMA((5,))],
        cost_estimate=pl.CostEstimate(
            flops=2 * rows * (reach + rows) * width,
            bytes_accessed=8 << 20,
            transcendentals=rows * reach * heads,
        ),
        compiler_params=pltpu.CompilerParams(vmem_limit_bytes=32 << 20),
        name="scores",
    )(
        here,
        near,
        two,
        four,
        *[pltpu.with_memory_space_constraint(x, pltpu.HBM) for x in brought],
    )


def combine(weights, inverses, values, here, width):
    rows = values[0].shape[0]
    kv_heads = values[0].shape[1] // HEAD_DIM
    group = width // values[0].shape[1]
    whole = pl.BlockSpec(memory_space=pltpu.VMEM)
    return pl.pallas_call(
        functools.partial(values_kernel, kv_heads, group),
        in_specs=[pl.BlockSpec(memory_space=pltpu.SMEM)] + [whole] * 8,
        out_specs=pl.BlockSpec(memory_space=pltpu.HBM),
        out_shape=jax.ShapeDtypeStruct((rows, width), jnp.bfloat16),
        scratch_shapes=[
            pltpu.VMEM((rows, width), jnp.bfloat16),
            pltpu.SemaphoreType.DMA((kv_heads,)),
        ],
        cost_estimate=pl.CostEstimate(
            flops=2 * rows * (BACK + 1) * rows * width, bytes_accessed=8 << 20, transcendentals=0
        ),
        compiler_params=pltpu.CompilerParams(vmem_limit_bytes=32 << 20),
        name="values",
    )(here, weights, inverses, *values)


def local(queries, keys, values, doc_start):
    rows, width = queries.shape
    devices = lax.axis_size(AXES)
    me = lax.axis_index(AXES)
    here = jnp.stack([me * rows, me % 2]).astype(jnp.int32)
    chain = devices - BACK

    def shifted(x, by):
        pairs = [(i, (i + by) % chain) for i in range(chain)]
        pairs += [(chain + i, chain + (i + 2) % BACK) for i in range(BACK)]
        return lax.ppermute(x, AXES, pairs)

    def four_back(x):
        return lax.ppermute(x, AXES, [(i, i + 4) for i in range(chain - 4)])

    def swapped(x):
        return lax.ppermute(x, AXES, [(i, i ^ 1) for i in range(devices)])

    key_near = swapped(keys)
    key_two, key_four = shifted(keys, 2), four_back(keys)
    value_two, value_four = shifted(values, 2), four_back(values)
    value_near = swapped(values)
    key_two_swap, key_four_swap = lax.cond(
        doc_start[0] >= 0,
        lambda a, b: (swapped(a), swapped(b)),
        lambda a, b: (a, b),
        key_two,
        key_four,
    )
    all_keys = (keys, key_near, key_two, key_two_swap, key_four, key_four_swap)
    weights, inverses, logs = weigh(queries, all_keys, doc_start, here)
    value_two, value_four, weights = lax.optimization_barrier((value_two, value_four, weights))
    all_values = (
        values, value_near, value_two, swapped(value_two), value_four, swapped(value_four)
    )
    return combine(weights, inverses, all_values, here, width), logs


def solution(mesh):
    placed = (P(AXES, None), P(AXES, None), P(AXES, None), P(AXES))
    return jax.shard_map(
        local,
        mesh=mesh,
        in_specs=placed,
        out_specs=(P(AXES, None), P(None, AXES)),
        check_vma=False,
    )
```

```python
import functools
import math

import jax
import jax.numpy as jnp
from jax import lax
from jax.experimental import pallas as pl
from jax.experimental.pallas import tpu as pltpu
from jax.sharding import PartitionSpec as P

HEAD_DIM = 128
BACK = 4
LOWEST = -1e30
SCALE = 1.0 / math.sqrt(HEAD_DIM)
LOG2E = math.log2(math.e)
AXES = ("seg", "dev")


def causal_tile(rows):
    key = lax.broadcasted_iota(jnp.int32, (rows, rows), 0)
    query = lax.broadcasted_iota(jnp.int32, (rows, rows), 1)
    return key <= query, key


def in_order(here_ref, blocks, at):
    own, near, two, two_swap, four, four_swap = (b[:, at] for b in blocks)
    odd = jnp.full(own.shape, here_ref[1], jnp.int32) == 1
    one = jnp.where(odd, near, two_swap)
    three = jnp.where(odd, two_swap, four_swap)
    return jnp.concatenate([own, four, one, two, three], axis=0)


def scores_kernel(
    pairs, group, here_ref, near, two, four, doc_hbm, q_hbm, own_hbm, two_swap_hbm, four_swap_hbm,
    weight_ref, inverse_ref, log_ref, doc_ref, q_ref, own, two_swap, four_swap, bias_ref, sems,
):
    moves = [
        (doc_hbm, doc_ref),
        (own_hbm, own),
        (two_swap_hbm, two_swap),
        (four_swap_hbm, four_swap),
        (q_hbm, q_ref),
    ]
    copies = [
        pltpu.make_async_copy(source, target, sems.at[index])
        for index, (source, target) in enumerate(moves)
    ]
    for copy in copies:
        copy.start()
    rows = q_ref.shape[0]
    causal, place = causal_tile(rows)
    copies[0].wait()
    start = jnp.broadcast_to(doc_ref[...] - here_ref[0], (rows, rows))
    merged = jnp.where(causal, place, place - BACK * rows)
    bias_ref[0] = jnp.where(merged >= start, 0.0, LOWEST)
    for back in range(1, BACK):
        bias_ref[back] = jnp.where(place - back * rows >= start, 0.0, LOWEST)
    for copy in copies[1:]:
        copy.wait()

    blocks = (own, near, two, two_swap, four, four_swap)
    for pair in range(pairs):
        key = in_order(here_ref, blocks, slice(pair * HEAD_DIM, (pair + 1) * HEAD_DIM))
        for g in range(group):
            head = pair * group + g
            raw = lax.dot_general(
                key,
                q_ref[:, head * HEAD_DIM : (head + 1) * HEAD_DIM],
                (((1,), (1,)), ((), ())),
                preferred_element_type=jnp.float32,
            )
            tiles = [jnp.where(causal, raw[:rows], raw[rows : 2 * rows]) + bias_ref[0]] + [
                raw[(back + 1) * rows : (back + 2) * rows] + bias_ref[back]
                for back in range(1, BACK)
            ]
            top = jnp.max(functools.reduce(jnp.maximum, tiles), axis=0, keepdims=True)
            expos = [jnp.exp2((tile - top) * (SCALE * LOG2E)) for tile in tiles]
            total = jnp.sum(functools.reduce(jnp.add, expos), axis=0, keepdims=True)
            for index, e in enumerate(expos):
                weight_ref[
                    (pair * BACK + index) * rows : (pair * BACK + index + 1) * rows,
                    g * rows : (g + 1) * rows,
                ] = e.astype(jnp.bfloat16)
            log_ref[head : head + 1] = top * SCALE + jnp.log(total)
            inverse_ref[head : head + 1] = 1.0 / total


def values_kernel(pairs, group, here_ref, weight_ref, inverse_ref, *refs):
    blocks, (out_hbm, out_ref, sems) = refs[:6], refs[6:]
    rows = out_ref.shape[0]
    copies = []
    causal, _ = causal_tile(rows)
    causal = jnp.concatenate([causal] * group, axis=1)
    for pair in range(pairs):
        value = in_order(here_ref, blocks, slice(pair * HEAD_DIM, (pair + 1) * HEAD_DIM))
        weights = weight_ref[pair * BACK * rows : (pair + 1) * BACK * rows]
        near = weights[:rows]
        zero = jnp.zeros_like(near)
        weights = jnp.concatenate(
            [jnp.where(causal, near, zero), jnp.where(causal, zero, near), weights[rows:]], axis=0
        )
        summed = lax.dot_general(
            value, weights, (((0,), (0,)), ((), ())), preferred_element_type=jnp.float32
        )
        for g in range(group):
            head = pair * group + g
            out_ref[:, head * HEAD_DIM : (head + 1) * HEAD_DIM] = jnp.transpose(
                (summed[:, g * rows : (g + 1) * rows] * inverse_ref[head : head + 1]).astype(
                    out_ref.dtype
                )
            )
        part = pl.ds(pair * group * HEAD_DIM, group * HEAD_DIM)
        copies.append(
            pltpu.make_async_copy(out_ref.at[:, part], out_hbm.at[:, part], sems.at[pair])
        )
        copies[-1].start()
    for copy in copies:
        copy.wait()


def weigh(queries, keys, doc_start, here):
    rows, width = queries.shape
    kv_heads = keys[0].shape[1] // HEAD_DIM
    group = width // keys[0].shape[1]
    heads = kv_heads * group
    reach = BACK * rows
    whole = pl.BlockSpec(memory_space=pltpu.VMEM)
    left = pl.BlockSpec(memory_space=pltpu.HBM)
    own, near, two, two_swap, four, four_swap = keys
    brought = [doc_start.reshape(1, rows), queries, own, two_swap, four_swap]
    return pl.pallas_call(
        functools.partial(scores_kernel, kv_heads, group),
        in_specs=[pl.BlockSpec(memory_space=pltpu.SMEM)] + [whole] * 3 + [left] * 5,
        out_specs=[whole] * 3,
        out_shape=[
            jax.ShapeDtypeStruct((kv_heads * reach, group * rows), jnp.bfloat16),
            jax.ShapeDtypeStruct((heads, rows), jnp.float32),
            jax.ShapeDtypeStruct((heads, rows), jnp.float32),
        ],
        scratch_shapes=[pltpu.VMEM(x.shape, x.dtype) for x in brought]
        + [pltpu.VMEM((BACK, rows, rows), jnp.float32), pltpu.SemaphoreType.DMA((5,))],
        cost_estimate=pl.CostEstimate(
            flops=2 * rows * (reach + rows) * width,
            bytes_accessed=8 << 20,
            transcendentals=rows * reach * heads,
        ),
        compiler_params=pltpu.CompilerParams(vmem_limit_bytes=32 << 20),
        name="scores",
    )(
        here,
        near,
        two,
        four,
        *[pltpu.with_memory_space_constraint(x, pltpu.HBM) for x in brought],
    )


def combine(weights, inverses, values, here, width):
    rows = values[0].shape[0]
    kv_heads = values[0].shape[1] // HEAD_DIM
    group = width // values[0].shape[1]
    whole = pl.BlockSpec(memory_space=pltpu.VMEM)
    return pl.pallas_call(
        functools.partial(values_kernel, kv_heads, group),
        in_specs=[pl.BlockSpec(memory_space=pltpu.SMEM)] + [whole] * 8,
        out_specs=pl.BlockSpec(memory_space=pltpu.HBM),
        out_shape=jax.ShapeDtypeStruct((rows, width), jnp.bfloat16),
        scratch_shapes=[
            pltpu.VMEM((rows, width), jnp.bfloat16),
            pltpu.SemaphoreType.DMA((kv_heads,)),
        ],
        cost_estimate=pl.CostEstimate(
            flops=2 * rows * (BACK + 1) * rows * width, bytes_accessed=8 << 20, transcendentals=0
        ),
        compiler_params=pltpu.CompilerParams(vmem_limit_bytes=32 << 20),
        name="values",
    )(here, weights, inverses, *values)


def local(queries, keys, values, doc_start):
    rows, width = queries.shape
    devices = lax.axis_size(AXES)
    me = lax.axis_index(AXES)
    here = jnp.stack([me * rows, me % 2]).astype(jnp.int32)
    chain = devices - BACK

    def shifted(x, by):
        pairs = [(i, (i + by) % chain) for i in range(chain)]
        pairs += [(chain + i, chain + (i + 2) % BACK) for i in range(BACK)]
        return lax.ppermute(x, AXES, pairs)

    def four_back(x):
        return lax.ppermute(x, AXES, [(i, i + 4) for i in range(chain - 4)])

    def swapped(x):
        return lax.ppermute(x, AXES, [(i, i ^ 1) for i in range(devices)])

    key_near = swapped(keys)
    key_two, key_four = shifted(keys, 2), four_back(keys)
    value_two, value_four = shifted(values, 2), four_back(values)
    value_near = swapped(values)
    key_two_swap, key_four_swap = lax.cond(
        doc_start[0] >= 0,
        lambda a, b: (swapped(a), swapped(b)),
        lambda a, b: (a, b),
        key_two,
        key_four,
    )
    all_keys = (keys, key_near, key_two, key_two_swap, key_four, key_four_swap)
    weights, inverses, logs = weigh(queries, all_keys, doc_start, here)
    value_four, weights = lax.optimization_barrier((value_four, weights))
    value_four_swap = swapped(value_four)
    value_two, value_four_swap = lax.optimization_barrier((value_two, value_four_swap))
    all_values = (
        values, value_near, value_two, swapped(value_two), value_four, value_four_swap
    )
    return combine(weights, inverses, all_values, here, width), logs


def solution(mesh):
    placed = (P(AXES, None), P(AXES, None), P(AXES, None), P(AXES))
    return jax.shard_map(
        local,
        mesh=mesh,
        in_specs=placed,
        out_specs=(P(AXES, None), P(None, AXES)),
        check_vma=False,
    )
```
